32 devices in a mesh: groups: 2 (over x), seq: 8 (over z, y), dec: 2 (over core).
Axes of the slice: x: 2, y: 2, z: 4, core: 2. Of those that a mesh axis runs over, the one named last changes fastest.
Arguments:
- tokens: bfloat16 [2048, 4096], P(('groups', 'seq')), parts along dimension 0, may hold values from -64 to 64
- norm_gain: float32 [4096], replicated, may hold values from 0.25 to 1.75
- w_query: bfloat16 [4096, 2048], P('seq', 'dec'), may hold values from -0.140625 to 0.140625
- w_key: bfloat16 [4096, 512], P('seq', 'dec'), may hold values from -0.140625 to 0.140625
- w_value: bfloat16 [4096, 512], P('seq', 'dec'), may hold values from -0.09375 to 0.09375
- block_order: int32 [32], P('groups'), parts along dimension 0, may hold values from 0 to 15, as said below
- block_docs: int32 [32], P('groups'), parts along dimension 0, may hold values from 0 to 3, never falling along the last dimension, each value on 1 to 8 neighbouring positions
- head_owner: int32 [8], P('groups'), parts along dimension 0, may hold values from 0 to 3, as said below
- prev_kv: bfloat16 [2048, 2, 4, 128], P(('groups', 'seq', 'dec')), parts along dimension 0, may hold values from -6 to 6
Outputs:
- attended: bfloat16 [2048, 2048], P(('groups', 'seq'), 'dec'), parts along dimension 0
- decode_cache: bfloat16 [2048, 2, 4, 128], P(('groups', 'seq'), None, 'dec'), parts along dimension 0
The draws below stay inside these ranges and needn't reach their ends.
There are 2 independent parts, one for each index of `groups`. The reference program is written for one: setup_inputs(seed, part) draws one part's arguments, and reference() takes and returns one part's arrays. A program takes and returns all parts, laid end to end along the dimension named above; an argument that names none is the same for every part. Nothing has to cross between parts.
Inputs may be any that keep to these rules, and one draw needn't show every extreme that they name: `block_order`: cycle slots 2i and 2i + 1 hold the blocks b and 15 - b for some b; every block stands in exactly one slot. `head_owner`: each key-value head stands in exactly one decode slot.
All inputs are finite; a program needn't handle non-finite values.
Results may differ from the reference program's by a relative error of at most 0.0035.
The reference program's roundings to bfloat16 on the way (of `normed`, `values` and `probability`) count: a program that leaves them out, or rounds other values in their place, can miss the bound.
Values may be sent and summed in bfloat16 or wider, within the bound.
No kernel may reach another device: no remote copies, remote signals or barrier semaphores. Data moves between devices by JAX's collectives and lax.ppermute only.
A program may use at most 64 MiB of HBM per device.

```python
import math
import jax
import jax.numpy as jnp
import numpy as np
from jax import lax

D = 4096
QH = 16
KVH = 4
HD = 128
TOKENS = 1024
BLK = 64
BLOCKS = 16
N_SEQ = 8


def query_base(key):
    return 3.0 * jax.random.truncated_normal(jax.random.fold_in(key, 11), -6.0, 6.0, (D, QH * HD), jnp.float32) / math.sqrt(D)


def draw_w_query(key, part):
    bound = 9.0 / math.sqrt(D)
    return jnp.clip(query_base(key), -bound, bound).astype(jnp.bfloat16)


def draw_w_key(key, part):
    bound = 9.0 / math.sqrt(D)
    fresh = jax.random.truncated_normal(jax.random.fold_in(key, 12), -6.0, 6.0, (D, KVH, HD), jnp.float32) / math.sqrt(D)
    return jnp.clip(fresh.reshape(D, KVH * HD), -bound, bound).astype(jnp.bfloat16)


def draw_tokens(key, part):
    base = jax.random.truncated_normal(jax.random.fold_in(key, 31), -6.0, 6.0, (TOKENS, D), jnp.float32)
    return base.astype(jnp.bfloat16)


def draw_block_order(key, part):
    pairs = BLOCKS // 2
    owner = jax.random.permutation(jax.random.fold_in(key, 21), pairs)
    flipped = jax.random.randint(jax.random.fold_in(key, 22), (pairs,), 0, 2)
    lower_block = owner
    upper_block = BLOCKS - 1 - owner
    leading = jnp.where(flipped == 1, upper_block, lower_block)
    trailing = jnp.where(flipped == 1, lower_block, upper_block)
    return jnp.stack([leading, trailing], 1).reshape(BLOCKS).astype(jnp.int32)


def draw_head_owner(key, part):
    return jax.random.permutation(jax.random.fold_in(key, 41), KVH).astype(jnp.int32)


def block_scale(rng, extent, pieces, smallest, high):
    level = 1.0
    for dim, blocks in pieces:
        draws = jax.random.uniform(jax.random.fold_in(jax.random.fold_in(rng, 6), dim), (blocks,), jnp.float32, smallest / len(pieces), high / len(pieces))
        level = level * jnp.repeat(jnp.exp(draws), extent[dim] // blocks).reshape((-1,) + (1,) * (len(extent) - 1 - dim))
    return level


def length_profile(number_of, total, limit, lean):
    loads = [(1 << 20) // math.isqrt(grade ** lean) + 1 for grade in range(2, number_of + 1)]
    surplus, given = total - limit - (number_of - 1), [1] * (number_of - 1)
    while surplus > 0:
        movable = [i for i in range(number_of - 1) if given[i] < limit]
        pool, budget = sum([loads[i] for i in movable]), surplus
        for i in movable:
            extra = min(limit - given[i], max(1, budget * loads[i] // pool), surplus)
            given[i] = given[i] + extra
            surplus = surplus - extra
    return np.array([limit] + given)


def ragged_sizes(own_key, number_of, total, most, slope):
    if number_of == 2:
        one = jax.random.randint(own_key, (), max(1, total - most), min(most, total - 1) + 1)
        return jnp.stack([one, total - one])
    sizes = jnp.asarray(length_profile(number_of, total, most, slope), jnp.int32)
    couples = (number_of - 1) // 2
    source_of, sink = sizes[1:1 + 2 * couples:2], sizes[2:2 + 2 * couples:2]
    slack = jnp.minimum(source_of - 1, most - sink)
    moved = jax.random.randint(jax.random.fold_in(own_key, 1), (couples,), 0, 1 << 20) % (slack + 1)
    sizes = sizes.at[1:1 + 2 * couples:2].set(source_of - moved).at[2:2 + 2 * couples:2].set(sink + moved)
    return sizes[jax.random.permutation(jax.random.fold_in(own_key, 2), number_of)]


def bell_draw(key, extent, width, limit, shards=(), kind=jnp.bfloat16):
    values = width * jax.random.normal(key, extent, jnp.float32)
    if shards:
        values = values * block_scale(key, extent, shards, -0.22, 0.18)
    return jnp.clip(values, -limit, limit).astype(kind)


def setup_inputs(seed: int = 0, part: int = 0) -> dict:
    key_list = jax.random.split(jax.random.key(seed), 10)
    part_keys = jax.random.split(jax.random.fold_in(key_list[9], part), 10)
    tokens = draw_tokens(jax.random.fold_in(jax.random.fold_in(key_list[9], part), 71), part)
    norm_gain = jnp.clip(1.0 + 0.15 * jax.random.normal(key_list[1], (D,), jnp.float32), 0.25, 1.75)
    w_query = draw_w_query(jax.random.fold_in(key_list[9], 71), part)
    w_key = draw_w_key(jax.random.fold_in(key_list[9], 71), part)
    w_value = bell_draw(key_list[4], (D, KVH * HD), D ** -0.5, 0.09375, ((0, 8), (1, 2)))
    block_order = draw_block_order(jax.random.fold_in(jax.random.fold_in(key_list[9], part), 71), part)
    block_docs = jnp.searchsorted(jnp.cumsum(ragged_sizes(part_keys[6], N_SEQ // 2, BLOCKS, N_SEQ, 2)), jnp.arange(BLOCKS), side="right").astype(jnp.int32)
    head_owner = draw_head_owner(jax.random.fold_in(jax.random.fold_in(key_list[9], part), 71), part)
    prev_kv = bell_draw(part_keys[8], (TOKENS, 2, KVH, HD), 1.0, 6.0, ((0, 16),))
    return dict(tokens=tokens, norm_gain=norm_gain, w_query=w_query, w_key=w_key, w_value=w_value, block_order=block_order, block_docs=block_docs, head_owner=head_owner, prev_kv=prev_kv)


def rotate(values, positions):
    half_width = values.shape[-1] // 2
    frequency = 500000.0 ** (-jnp.arange(half_width, dtype=jnp.float32) / half_width)
    angles = positions[:, None].astype(jnp.float32) * frequency[None, :]
    cosines = jnp.cos(angles)[:, None, :]
    sine_terms = jnp.sin(angles)[:, None, :]
    lower_half = values[..., :half_width]
    upper_half = values[..., half_width:]
    return jnp.concatenate([lower_half * cosines - upper_half * sine_terms, upper_half * cosines + lower_half * sine_terms], -1)

def reference(tokens, norm_gain, w_query, w_key, w_value, block_order, block_docs, head_owner, prev_kv):
    inputs = tokens.astype(jnp.float32)
    normed = (inputs * lax.rsqrt(lax.optimization_barrier(jnp.mean(inputs * inputs, -1, keepdims=True)) + 1e-05) * norm_gain).astype(jnp.bfloat16)
    row_ids = jnp.arange(TOKENS, dtype=jnp.int32)
    natural = block_order[row_ids // BLK]
    positions = natural * BLK + row_ids % BLK
    documents = block_docs[natural]
    queries = rotate(jnp.dot(normed, w_query, preferred_element_type=jnp.float32).reshape(TOKENS, QH, HD), positions).astype(jnp.bfloat16)
    key_rows = rotate(jnp.dot(normed, w_key, preferred_element_type=jnp.float32).reshape(TOKENS, KVH, HD), positions).astype(jnp.bfloat16)
    value_rows = jnp.dot(normed, w_value, preferred_element_type=jnp.float32).astype(jnp.bfloat16).reshape(TOKENS, KVH, HD)
    allowed = (positions[None, :] <= positions[:, None]) & (documents[None, :] == documents[:, None])
    group_size = QH // KVH
    scale = 1.0 / math.sqrt(HD)

    def one_head(head_index):
        query_head = queries[:, head_index]
        key_head = key_rows[:, head_index // group_size]
        value_head = value_rows[:, head_index // group_size]
        scores = jnp.dot(query_head, key_head.T, preferred_element_type=jnp.float32) * scale
        scores = jnp.where(allowed, scores, -jnp.inf)
        row_max = lax.optimization_barrier(jnp.max(scores, -1, keepdims=True))
        exponent_terms = jnp.exp(scores - row_max)
        running_sum = lax.optimization_barrier(jnp.sum(exponent_terms, -1, keepdims=True))
        probability = exponent_terms.astype(jnp.bfloat16)
        return jnp.dot(probability, value_head, preferred_element_type=jnp.float32) / running_sum
    heads_out = lax.map(one_head, jnp.arange(QH, dtype=jnp.int32))
    attended = jnp.transpose(heads_out, (1, 0, 2)).reshape(TOKENS, QH * HD).astype(jnp.bfloat16)
    decode_cache = prev_kv[:, :, head_owner, :]
    return (attended, decode_cache)
```

```python
import functools
import math

import jax
import jax.numpy as jnp
from jax import lax
from jax.experimental import pallas as pl
from jax.experimental.pallas import tpu as pltpu
from jax.sharding import PartitionSpec as P

HD = 128


def project_kernel(n_tok, n_blk, first, last, depth, kidx, dst, nat, *refs):
    toks = refs[:n_tok]
    blks = refs[n_tok : n_tok + n_blk]
    rest = list(refs[n_tok + n_blk :])
    acc = None if first else rest.pop(0)[...]
    for s in range(n_blk):
        cols = pl.ds(pl.multiple_of(kidx[s] * depth, depth), depth)
        lhs = jnp.concatenate([t[:, cols] for t in toks], axis=0)
        part = jnp.dot(lhs, blks[s][...], preferred_element_type=jnp.float32)
        acc = part if acc is None else acc + part
    if not last:
        rest[0][...] = acc
        return
    cos_ref, sin_ref, out = rest
    rotated = nat[nat.shape[0] - 1] == 0
    block = out.shape[1]
    heads = out.shape[2] // HD
    for k in range(out.shape[0]):
        c, s = cos_ref[nat[k]], sin_ref[nat[k]]
        for h in range(heads):
            v = acc[k * block : (k + 1) * block, h * HD : (h + 1) * HD]
            r = v * c + pltpu.roll(v, HD // 2, 1) * s
            if h == heads - 1:
                r = jnp.where(rotated, r, v)
            out[dst[k], :, h * HD : (h + 1) * HD] = r.astype(jnp.bfloat16)


def project(kidx, dst, nat, toks, blks, acc, tables, out_shape):
    first, last = acc is None, tables is not None
    depth = blks[0].shape[0]
    args = list(toks) + list(blks)
    if not first:
        args.append(acc)
    if last:
        args.extend(tables)
    smem = pl.BlockSpec(memory_space=pltpu.SMEM)
    vmem = pl.BlockSpec(memory_space=pltpu.VMEM)
    rows = sum(t.shape[0] for t in toks)
    flops = 2 * rows * depth * len(blks) * blks[0].shape[1]
    return pl.pallas_call(
        functools.partial(project_kernel, len(toks), len(blks), first, last, depth),
        out_shape=out_shape,
        in_specs=[smem] * 3 + [vmem] * len(args),
        out_specs=vmem,
        cost_estimate=pl.CostEstimate(
            flops=flops, bytes_accessed=sum(a.size * a.dtype.itemsize for a in args), transcendentals=0
        ),
        name="project_last" if last else "project_first",
    )(kidx, dst, nat, *args)


def attend_kernel(group_size, scale, qnat, qdoc, kpos_ref, kdoc_ref, low, high, *refs):
    kvs, out = refs[:-1], refs[-1]
    kpos, kdoc = kpos_ref[...], kdoc_ref[...]
    blocks, block, width = low.shape
    q_heads = width // HD - 1
    key = jnp.concatenate([r[0] for r in kvs], axis=0)
    value = jnp.concatenate([r[1] for r in kvs], axis=0)
    for k in range(blocks):
        query = jnp.concatenate(
            [r[k, :, h * HD : (h + 1) * HD] for r in (low, high) for h in range(q_heads)], axis=0
        )
        scores = (
            lax.dot_general(query, key, (((1,), (1,)), ((), ())), preferred_element_type=jnp.float32)
            * scale
        )
        qpos = qnat[k] * block + lax.broadcasted_iota(jnp.int32, (block, 1), 0)
        allowed = (kpos <= qpos) & (kdoc == qdoc[k])
        bias = jnp.where(allowed, 0.0, -jnp.inf)
        scores = scores + jnp.concatenate([bias] * group_size, axis=0)
        row_max = jnp.max(scores, axis=-1, keepdims=True)
        weights = jnp.exp(scores - row_max)
        total = jnp.sum(weights, axis=-1, keepdims=True)
        mixed = jnp.dot(weights.astype(jnp.bfloat16), value, preferred_element_type=jnp.float32) / total
        for h in range(group_size):
            out[k * block : (k + 1) * block, h * HD : (h + 1) * HD] = mixed[
                h * block : (h + 1) * block
            ].astype(jnp.bfloat16)


def per_device(
    tokens, norm_gain, w_query, w_key, w_value, block_order, block_docs, head_owner, prev_kv
):
    groups, n_seq = lax.axis_size("groups"), lax.axis_size("seq")
    planes = n_seq // 2
    rows_dev = tokens.shape[0]
    depth = w_query.shape[0]
    slots = block_order.shape[0] // n_seq
    block = rows_dev // slots
    local_kv = w_key.shape[1] // HD
    local_heads = w_query.shape[1] // HD
    group_size = local_heads // local_kv
    g, i, c = lax.axis_index("groups"), lax.axis_index("seq"), lax.axis_index("dec")
    x = g % 2
    b = (i // 2) % 2

    def swap_seq(v, mask):
        return lax.ppermute(v, "seq", [(j, j ^ mask) for j in range(n_seq)])

    def swap_group(v):
        return lax.ppermute(v, "groups", [(j, j ^ 1) for j in range(groups)])

    def swap_core(v):
        return lax.ppermute(v, "dec", [(0, 1), (1, 0)])

    tables_own = jnp.stack([block_order, block_docs])
    tables_other = swap_group(tables_own)
    tables_abs = jnp.stack(
        [jnp.where(x == 0, tables_own, tables_other), jnp.where(x == 0, tables_other, tables_own)]
    )

    inputs = tokens.astype(jnp.float32)
    normed = (
        inputs * lax.rsqrt(jnp.mean(inputs * inputs, -1, keepdims=True) + 1e-05) * norm_gain
    ).astype(jnp.bfloat16)
    half = lax.dynamic_slice_in_dim(normed, c * block, block, 0)

    q_cols = w_query.shape[1] // 4

    def columns(parity):
        query = lax.dynamic_slice_in_dim(w_query, (x * 2 + parity) * q_cols, q_cols, 1)
        keys = lax.dynamic_slice_in_dim(w_key, x * HD, HD, 1)
        values = lax.dynamic_slice_in_dim(w_value, x * HD, HD, 1)
        return jnp.concatenate([query, jnp.where(parity == 0, keys, values)], axis=1)

    same, other = columns(b), columns(1 - b)

    tok_z = swap_seq(half, 2)
    tok_x = swap_group(half)
    arrived = {0: same}
    for d in range(planes - 1, 0, -1):
        arrived[2 * d] = swap_seq(other if d % 2 else same, 2 * d)
    for d in range(planes):
        arrived[2 * d + 1] = swap_seq(arrived[2 * d], 1)
    tok_xz = swap_group(tok_z)
    toks = [normed, tok_z, tok_x, tok_xz] + [swap_core(t) for t in (tok_z, tok_x, tok_xz)]

    grp = jnp.stack([x, x, x, 1 - x, 1 - x, x, 1 - x, 1 - x])
    par = jnp.stack([b, b, 1 - b, b, 1 - b, 1 - b, b, 1 - b])
    part = jnp.stack([0 * c, 0 * c + 1, c, c, c, 1 - c, 1 - c, 1 - c])
    base = i - 2 * b
    slot = (base + 2 * par) * slots + part

    def pick(table, index):
        hot = index[:, None] == jnp.arange(table.shape[0], dtype=jnp.int32)[None, :]
        return jnp.sum(jnp.where(hot, table[None, :], 0), axis=1)

    orders = tables_abs[:, 0].reshape(-1)
    nat = pick(orders, grp * block_order.shape[0] + slot)
    nat = jnp.concatenate([nat, b[None]])
    dst = jnp.where(grp == b, 0, 4) + par * 2 + part

    n_blocks = block_order.shape[0]
    frequency = 500000.0 ** (-jnp.arange(HD // 2, dtype=jnp.float32) / (HD // 2))
    angles = jnp.arange(n_blocks * block, dtype=jnp.int32).astype(jnp.float32)[:, None] * frequency[None, :]
    cosines, sines = jnp.cos(angles), jnp.sin(angles)
    cos_table = jnp.concatenate([cosines, cosines], -1).reshape(n_blocks, block, HD)
    sin_table = jnp.concatenate([-sines, sines], -1).reshape(n_blocks, block, HD)

    late = [2, 3] if planes == 2 else [4, 5]
    early = [m for m in range(n_seq) if m not in late]

    def ids(masks):
        return jnp.stack([i ^ m for m in masks])

    width = same.shape[1]
    total_rows = 8 * block
    acc = project(
        ids(early), dst, nat, toks, [arrived[m] for m in early], None, None,
        jax.ShapeDtypeStruct((total_rows, width), jnp.float32),
    )
    mine = project(
        ids(late), dst, nat, toks, [arrived[m] for m in late], acc, (cos_table, sin_table),
        jax.ShapeDtypeStruct((8, block, width), jnp.bfloat16),
    )
    keep, give = mine[:4], mine[4:]
    got = swap_seq(give, 2)
    low = jnp.where(b == 0, keep, got)
    high = jnp.where(b == 0, got, keep)
    own_kv = jnp.stack([low[:, :, -HD:], high[:, :, -HD:]]).reshape(2, 4 * block, HD)
    masks = [4 * (m // 2) + m % 2 for m in range(n_seq // 2)]
    kvs = [own_kv] + [swap_seq(own_kv, m) for m in masks[1:]]

    order_b = jnp.where(b == 0, tables_abs[0, 0], tables_abs[1, 0])
    docs_b = jnp.where(b == 0, tables_abs[0, 1], tables_abs[1, 1])
    inner = jnp.arange(4, dtype=jnp.int32)
    q_slot = (base + 2 * (inner // 2)) * slots + inner % 2
    k_slot = jnp.concatenate([((base ^ m) + 2 * (inner // 2)) * slots + inner % 2 for m in masks])
    q_nat = pick(order_b, q_slot)
    q_doc = pick(docs_b, q_nat)
    k_nat = pick(order_b, k_slot)
    k_doc = pick(docs_b, k_nat)
    row = jnp.arange(block, dtype=jnp.int32)
    k_pos = (k_nat[:, None] * block + row[None, :]).reshape(1, -1)
    k_doc = jnp.broadcast_to(k_doc[:, None], (k_doc.shape[0], block)).reshape(1, -1)

    smem = pl.BlockSpec(memory_space=pltpu.SMEM)
    vmem = pl.BlockSpec(memory_space=pltpu.VMEM)
    attended = pl.pallas_call(
        functools.partial(attend_kernel, group_size, 1.0 / math.sqrt(HD)),
        out_shape=jax.ShapeDtypeStruct((4 * block, group_size * HD), jnp.bfloat16),
        in_specs=[smem] * 2 + [vmem] * (4 + len(kvs)),
        out_specs=vmem,
        name="attend",
    )(q_nat, q_doc, k_pos, k_doc, low, high, *kvs)

    first_rows = attended[:rows_dev]
    second_rows = attended[rows_dev:]
    at_b = jnp.where(b == 0, first_rows, second_rows)
    at_other = jnp.where(b == 0, second_rows, first_rows)
    perm_a, perm_b = [], []
    for gg in range(groups):
        for ii in range(n_seq):
            src = gg * n_seq + ii
            if gg % 2 == (ii // 2) % 2:
                perm_a.append((src, gg * n_seq + (ii ^ 2)))
            else:
                perm_a.append((src, (gg ^ 1) * n_seq + ii))
                perm_b.append((src, (gg ^ 1) * n_seq + (ii ^ 2)))
    home = x == b
    from_a = lax.ppermute(jnp.where(home, at_other, at_b), ("groups", "seq"), perm_a)
    from_b = lax.ppermute(at_other, ("groups", "seq"), perm_b)
    same_x = jnp.where(home, at_b, from_a)
    cross_x = jnp.where(home, from_a, from_b)
    out = jnp.concatenate(
        [jnp.where(x == 0, same_x, cross_x), jnp.where(x == 0, cross_x, same_x)], axis=1
    )

    head_count = prev_kv.shape[2]
    selector = (head_owner[:, None] == jnp.arange(head_count, dtype=jnp.int32)[None, :]).astype(
        jnp.bfloat16
    )
    ordered = jnp.einsum(
        "tcjd,sj->tcsd", prev_kv, selector, preferred_element_type=jnp.float32
    ).astype(jnp.bfloat16)
    per_dec = head_count // 2
    stay = jnp.where(c == 0, ordered[:, :, :per_dec], ordered[:, :, per_dec:])
    leave = jnp.where(c == 0, ordered[:, :, per_dec:], ordered[:, :, :per_dec])
    come = swap_core(leave)
    decode_cache = jnp.concatenate(
        [jnp.where(c == 0, stay, come), jnp.where(c == 0, come, stay)], axis=0
    )
    return (out, decode_cache)


def solution(mesh):
    in_specs = (
        P(("groups", "seq"), None),
        P(),
        P("seq", "dec"),
        P("seq", "dec"),
        P("seq", "dec"),
        P("groups"),
        P("groups"),
        P("groups"),
        P(("groups", "seq", "dec"), None, None, None),
    )
    out_specs = (P(("groups", "seq"), "dec"), P(("groups", "seq"), None, "dec", None))
    return jax.shard_map(
        per_device, mesh=mesh, in_specs=in_specs, out_specs=out_specs, check_vma=False
    )
```

```python
import functools
import math

import jax
import jax.numpy as jnp
from jax import lax
from jax.experimental import pallas as pl
from jax.experimental.pallas import tpu as pltpu
from jax.sharding import PartitionSpec as P


HD = 128
VMEM = pltpu.CompilerParams(vmem_limit_bytes=16 * 2**20)


def place():
    g, i, c = lax.axis_index("groups"), lax.axis_index("seq"), lax.axis_index("dec")
    return g % 2, i, lax.div(i, 2) % 2, c


def sources(order_own, order_other):
    x, i, b, c = place()
    found = []
    for k in range(8):
        grp = x if k % 4 < 2 else 1 - x
        par = b if k % 4 in (0, 2) else 1 - b
        part = c if k < 4 else 1 - c
        slot = (i - 2 * b + 2 * par) * 2 + part
        nat = order_own[slot] if k % 4 < 2 else order_other[slot]
        found.append((nat, grp == b, par * 2 + part))
    return found


def product(lhs_ref, index, blk, start, width):
    depth = blk.shape[0]
    cols = pl.ds(pl.multiple_of(index * depth, depth), depth)
    return jnp.dot(
        lhs_ref[:, cols], blk[:, start : start + width], preferred_element_type=jnp.float32
    )


def gather_kernel(n_tok, kv_masks, q_masks, order_own, order_other, *refs):
    _, i, _, _ = place()
    toks, refs = refs[:n_tok], refs[n_tok:]
    both, refs = refs[: len(q_masks)], refs[len(q_masks) :]
    kvs, refs = refs[: len(kv_masks)], refs[len(kv_masks) :]
    rope, rows, kv_sum, q_sum, spin = refs
    block = toks[0].shape[0]
    for n, tok in enumerate(toks):
        rows[n * block : (n + 1) * block, :] = tok[...]
    for k, (nat, _, _) in enumerate(sources(order_own, order_other)):
        spin[k] = rope[nat]
    width = both[0].shape[1]
    acc = None
    for blk, mask in zip(both, q_masks):
        part = product(rows, i ^ mask, blk, 0, width)
        acc = part if acc is None else acc + part
    q_sum[...] = acc[:, HD:]
    acc = acc[:, :HD]
    for blk, mask in zip(kvs, kv_masks):
        acc = acc + product(rows, i ^ mask, blk, 0, HD)
    kv_sum[...] = acc


def gather(toks, both, q_masks, kvs, kv_masks, orders, rope):
    smem = pl.BlockSpec(memory_space=pltpu.SMEM)
    vmem = pl.BlockSpec(memory_space=pltpu.VMEM)
    block, width = toks[0].shape
    rows = block * len(toks)
    q_width = both[0].shape[1] - HD
    args = list(toks) + list(both) + list(kvs) + [rope]
    return pl.pallas_call(
        functools.partial(gather_kernel, len(toks), kv_masks, q_masks),
        out_shape=[
            pltpu.VMEM((rows, width), jnp.bfloat16),
            pltpu.VMEM((rows, HD), jnp.float32),
            pltpu.VMEM((rows, q_width), jnp.float32),
            pltpu.VMEM((len(toks),) + rope.shape[1:], jnp.float32),
        ],
        in_specs=[smem] * 2 + [vmem] * len(args),
        out_specs=[vmem] * 4,
        compiler_params=VMEM,
        cost_estimate=pl.CostEstimate(flops=2**30, bytes_accessed=2**20, transcendentals=0),
        name="gather_rows",
    )(*orders, *args)


def project_kernel(masks, mode, order_own, order_other, rows, acc_ref, *refs):
    _, i, b, _ = place()
    blks, refs = refs[: len(masks)], refs[len(masks) :]
    acc = acc_ref[...]
    for blk, mask in zip(blks, masks):
        acc = acc + product(rows, i ^ mask, blk, 0, blk.shape[1])
    if mode == "part":
        refs[0][...] = acc
        return
    spin, keep, give = refs
    block, heads = keep.shape[1], keep.shape[2] // HD
    for k, (_, kept, spot) in enumerate(sources(order_own, order_other)):
        cos, sin = spin[k, 0], spin[k, 1]
        tiles = []
        for h in range(heads):
            v = acc[k * block : (k + 1) * block, h * HD : (h + 1) * HD]
            r = v * cos + pltpu.roll(v, HD // 2, 1) * sin
            if mode == "key_value":
                r = jnp.where(b == 0, r, v)
            tiles.append(r.astype(jnp.bfloat16))
        value = tiles[0] if heads == 1 else jnp.concatenate(tiles, axis=1)

        @pl.when(kept)
        def _():
            keep[spot] = value

        @pl.when(jnp.logical_not(kept))
        def _():
            give[spot] = value


def project(mode, rows, acc, blks, masks, orders, spin=None):
    smem = pl.BlockSpec(memory_space=pltpu.SMEM)
    vmem = pl.BlockSpec(memory_space=pltpu.VMEM)
    width = blks[0].shape[1]
    args = [rows, acc] + list(blks) + ([] if spin is None else [spin])
    if mode == "part":
        out_shape = [pltpu.VMEM(acc.shape, jnp.float32)]
    else:
        blocks, _, block, _ = spin.shape
        out_shape = [jax.ShapeDtypeStruct((blocks // 2, block, width), jnp.bfloat16)] * 2
    return pl.pallas_call(
        functools.partial(project_kernel, masks, mode),
        out_shape=out_shape,
        in_specs=[smem] * 2 + [vmem] * len(args),
        out_specs=[vmem] * len(out_shape),
        compiler_params=VMEM,
        cost_estimate=pl.CostEstimate(flops=2**30, bytes_accessed=2**20, transcendentals=0),
    )(*orders, *args)


def norm_kernel(tok, gain, normed):
    v = tok[...].astype(jnp.float32)
    scale = lax.rsqrt(jnp.mean(v * v, axis=-1, keepdims=True) + 1e-05)
    normed[...] = (v * scale * gain[...]).astype(jnp.bfloat16)


def norm(tokens, gain, block, index):
    width = tokens.shape[1]
    return pl.pallas_call(
        norm_kernel,
        grid=(1,),
        out_shape=jax.ShapeDtypeStruct((block, width), jnp.bfloat16),
        in_specs=[
            pl.BlockSpec((block, width), lambda n: (index(), 0)),
            pl.BlockSpec((1, width), lambda n: (0, 0)),
        ],
        out_specs=pl.BlockSpec((block, width), lambda n: (0, 0)),
        compiler_params=VMEM,
        name="norm",
    )(tokens, gain)


def attend_kernel(kv_masks, scale, *refs):
    x, i, b, _ = place()
    order_own, docs_own, order_other, docs_other, query_ref = refs[:5]
    kvs, outs = refs[5:-1], refs[-1:]
    blocks, block, width = query_ref.shape
    heads = width // HD

    def table(own, other, index):
        return jnp.where(x == b, own[index], other[index])

    base = i - 2 * b
    lane = lax.broadcasted_iota(jnp.int32, (1, 2 * block), 1)
    pos_parts, doc_parts = [], []
    for mask in kv_masks:
        for par in range(2):
            slot = ((base ^ mask) + 2 * par) * 2
            n0, n1 = table(order_own, order_other, slot), table(order_own, order_other, slot + 1)
            d0, d1 = table(docs_own, docs_other, n0), table(docs_own, docs_other, n1)
            pos_parts.append(jnp.where(lane < block, n0 * block, (n1 - 1) * block) + lane)
            doc_parts.append(jnp.where(lane < block, d0, d1))
    kpos, kdoc = jnp.concatenate(pos_parts, axis=1), jnp.concatenate(doc_parts, axis=1)
    keys, values = [], []
    for n in range(len(kv_masks)):
        for k in range(blocks):
            kept, got = kvs[2 * n][k], kvs[2 * n + 1][k]
            keys.append(jnp.where(b == 0, kept, got))
            values.append(jnp.where(b == 0, got, kept))
    key, value = jnp.concatenate(keys, axis=0), jnp.concatenate(values, axis=0)
    for k in range(blocks):
        par, part = k // 2, k % 2
        nat = table(order_own, order_other, (base + 2 * par) * 2 + part)
        doc = table(docs_own, docs_other, nat)
        query = jnp.concatenate([query_ref[k, :, h * HD : (h + 1) * HD] for h in range(heads)], axis=0)
        scores = (
            lax.dot_general(query, key, (((1,), (1,)), ((), ())), preferred_element_type=jnp.float32)
            * scale
        )
        qpos = nat * block + lax.broadcasted_iota(jnp.int32, (block, 1), 0)
        bias = jnp.where((kpos <= qpos) & (kdoc == doc), 0.0, -jnp.inf)
        scores = scores + jnp.concatenate([bias] * heads, axis=0)
        row_max = jnp.max(scores, axis=-1, keepdims=True)
        weights = jnp.exp(scores - row_max)
        total = jnp.sum(weights, axis=-1, keepdims=True)
        mixed = jnp.dot(weights.astype(jnp.bfloat16), value, preferred_element_type=jnp.float32) / total
        rows = jnp.concatenate(
            [mixed[h * block : (h + 1) * block].astype(jnp.bfloat16) for h in range(heads)], axis=1
        )
        outs[0][k * block : (k + 1) * block, :] = rows


def attend(tables, query, kvs, kv_masks):
    blocks, block, width = query.shape
    smem = pl.BlockSpec(memory_space=pltpu.SMEM)
    vmem = pl.BlockSpec(memory_space=pltpu.VMEM)
    return pl.pallas_call(
        functools.partial(attend_kernel, kv_masks, 1.0 / math.sqrt(HD)),
        out_shape=jax.ShapeDtypeStruct((blocks * block, width), jnp.bfloat16),
        in_specs=[smem] * len(tables) + [vmem] * (1 + len(kvs)),
        out_specs=vmem,
        compiler_params=VMEM,
        cost_estimate=pl.CostEstimate(flops=10**9, bytes_accessed=10**6, transcendentals=10**6),
    )(*tables, query, *kvs)


def per_device(
    tokens, norm_gain, w_query, w_key, w_value, block_order, block_docs, head_owner, prev_kv
):
    groups, n_seq = lax.axis_size("groups"), lax.axis_size("seq")
    planes = n_seq // 2
    rows_dev = tokens.shape[0]
    slots = block_order.shape[0] // n_seq
    block = rows_dev // slots
    x, _, b, c = place()

    def swap_seq(v, mask):
        return lax.ppermute(v, "seq", [(j, j ^ mask) for j in range(n_seq)])

    def swap_group(v):
        return lax.ppermute(v, "groups", [(j, j ^ 1) for j in range(groups)])

    def swap_core(v):
        return lax.ppermute(v, "dec", [(0, 1), (1, 0)])

    smem = pl.BlockSpec(memory_space=pltpu.SMEM)
    vmem = pl.BlockSpec(memory_space=pltpu.VMEM)
    gain = norm_gain[None, :]
    half = norm(tokens, gain, block, lambda: place()[3])
    rest = norm(tokens, gain, block, lambda: 1 - place()[3])

    n_blocks = block_order.shape[0]
    frequency = 500000.0 ** (-jnp.arange(HD // 2, dtype=jnp.float32) / (HD // 2))
    angles = jnp.arange(n_blocks * block, dtype=jnp.int32).astype(jnp.float32)[:, None] * frequency[None, :]
    cosines, sines = jnp.cos(angles), jnp.sin(angles)
    cos_table = jnp.concatenate([cosines, cosines], -1).reshape(n_blocks, 1, block, HD)
    sin_table = jnp.concatenate([-sines, sines], -1).reshape(n_blocks, 1, block, HD)
    rope = jnp.concatenate([cos_table, sin_table], axis=1)

    own_tables = jnp.concatenate([block_order, block_docs])
    own_tables, rope = lax.optimization_barrier((own_tables, rope))
    other_tables = swap_group(own_tables)
    order_other = other_tables[: block_order.shape[0]]
    docs_other = other_tables[block_order.shape[0] :]

    q_cols = w_query.shape[1] // 4
    keys = lax.dynamic_slice_in_dim(w_key, x * HD, HD, 1)
    values = lax.dynamic_slice_in_dim(w_value, x * HD, HD, 1)
    kv_cols = [jnp.where(b == 0, keys, values), jnp.where(b == 0, values, keys)]
    q_parts = [
        lax.dynamic_slice_in_dim(w_query, (x * 2 + parity) * q_cols, q_cols, 1)
        for parity in (b, 1 - b)
    ]

    tok_z = swap_seq(half, 2)
    tok_x = swap_group(half)
    near = jnp.concatenate([kv_cols[0], q_parts[0]], axis=1)
    both_y0 = swap_seq(near, 1)
    kv_z = [near] + [swap_seq(kv_cols[d % 2], 2 * d) for d in range(1, planes)]
    q_z = [near] + [swap_seq(q_parts[d % 2], 2 * d) for d in range(1, planes)]
    kv_y = [both_y0] + [swap_seq(kv_z[d], 1) for d in range(1, planes)]
    q_y = [both_y0] + [swap_seq(q_z[d], 1) for d in range(1, planes)]
    tok_xz = swap_group(tok_z)
    toks = [half, tok_z, tok_x, tok_xz, rest] + [swap_core(t) for t in (tok_z, tok_x, tok_xz)]

    orders = (block_order, order_other)

    rows, kv_acc, q_acc, spin = gather(
        toks, (near, both_y0), (0, 1), kv_z[1:], [2 * d for d in range(1, planes)], orders, rope
    )
    kv_keep, kv_give = project(
        "key_value", rows, kv_acc, kv_y[1:], [2 * d + 1 for d in range(1, planes)], orders, spin
    )
    kvx_z = [kv_keep] + [swap_seq(kv_give if d % 2 else kv_keep, 2 * d) for d in range(1, planes)]
    kvx_y = [swap_seq(kvx_z[d], 1) for d in range(planes)]
    pairs = range(0, planes, 2)
    kv_masks = [2 * d for d in pairs] + [2 * d + 1 for d in pairs]
    kv_all = [v for part in (kvx_z, kvx_y) for v in part]

    last = 2 if planes > 2 else 1
    (q_acc,) = project(
        "part", rows, q_acc,
        q_z[1:] + [q_y[d] for d in range(1, planes) if d != last],
        [2 * d for d in range(1, planes)] + [2 * d + 1 for d in range(1, planes) if d != last],
        orders,
    )
    q_keep, q_give = project(
        "query", rows, q_acc, [q_y[last]], [2 * last + 1], orders, spin
    )
    q_got = swap_seq(q_give, 2)

    tables = (block_order, block_docs, order_other, docs_other)
    att_keep = attend(tables, q_keep, kv_all, kv_masks)
    att_got = attend(tables, q_got, kv_all, kv_masks)
    att = [att_keep, att_got]
    attended = jnp.concatenate(
        [jnp.where(b == 0, att[0], att[1]), jnp.where(b == 0, att[1], att[0])], axis=1
    )

    first_rows = attended[:rows_dev]
    second_rows = attended[rows_dev:]
    at_b = jnp.where(b == 0, first_rows, second_rows)
    at_other = jnp.where(b == 0, second_rows, first_rows)
    perm_a, perm_b = [], []
    for gg in range(groups):
        for ii in range(n_seq):
            src = gg * n_seq + ii
            if gg % 2 == (ii // 2) % 2:
                perm_a.append((src, gg * n_seq + (ii ^ 2)))
            else:
                perm_a.append((src, (gg ^ 1) * n_seq + ii))
                perm_b.append((src, (gg ^ 1) * n_seq + (ii ^ 2)))
    home = x == b
    from_a = lax.ppermute(jnp.where(home, at_other, at_b), ("groups", "seq"), perm_a)
    from_b = lax.ppermute(at_other, ("groups", "seq"), perm_b)
    same_x = jnp.where(home, at_b, from_a)
    cross_x = jnp.where(home, from_a, from_b)
    out = jnp.concatenate(
        [jnp.where(x == 0, same_x, cross_x), jnp.where(x == 0, cross_x, same_x)], axis=1
    )

    head_count = prev_kv.shape[2]
    selector = (head_owner[:, None] == jnp.arange(head_count, dtype=jnp.int32)[None, :]).astype(
        jnp.bfloat16
    )
    ordered = jnp.einsum(
        "tcjd,sj->tcsd", prev_kv, selector, preferred_element_type=jnp.float32
    ).astype(jnp.bfloat16)
    per_dec = head_count // 2
    stay = jnp.where(c == 0, ordered[:, :, :per_dec], ordered[:, :, per_dec:])
    leave = jnp.where(c == 0, ordered[:, :, per_dec:], ordered[:, :, :per_dec])
    come = swap_core(leave)
    decode_cache = jnp.concatenate(
        [jnp.where(c == 0, stay, come), jnp.where(c == 0, come, stay)], axis=0
    )
    return (out, decode_cache)


def solution(mesh):
    in_specs = (
        P(("groups", "seq"), None),
        P(),
        P("seq", "dec"),
        P("seq", "dec"),
        P("seq", "dec"),
        P("groups"),
        P("groups"),
        P("groups"),
        P(("groups", "seq", "dec"), None, None, None),
    )
    out_specs = (P(("groups", "seq"), "dec"), P(("groups", "seq"), None, "dec", None))

    return jax.shard_map(
        per_device, mesh=mesh, in_specs=in_specs, out_specs=out_specs, check_vma=False
    )
```

```python
import functools
import math

import jax
import jax.numpy as jnp
from jax import lax
from jax.experimental import pallas as pl
from jax.experimental.pallas import tpu as pltpu
from jax.sharding import PartitionSpec as P


HD = 128
VMEM = pltpu.CompilerParams(vmem_limit_bytes=16 * 2**20)
CUT = None
COST = pl.CostEstimate(flops=1024, bytes_accessed=1024, transcendentals=0)


def place():
    g, i, c = lax.axis_index("groups"), lax.axis_index("seq"), lax.axis_index("dec")
    return g % 2, i, lax.div(i, 2) % 2, c


def sources(order_own, order_other):
    x, i, b, c = place()
    found = []
    for k in range(8):
        grp = x if k % 4 < 2 else 1 - x
        par = b if k % 4 in (0, 2) else 1 - b
        part = c if k < 4 else 1 - c
        slot = (i - 2 * b + 2 * par) * 2 + part
        nat = order_own[slot] if k % 4 < 2 else order_other[slot]
        found.append((nat, grp == b, par * 2 + part))
    return found


def product(lhs_ref, index, blk, start, width):
    depth = blk.shape[0]
    cols = pl.ds(pl.multiple_of(index * depth, depth), depth)
    return jnp.dot(
        lhs_ref[:, cols], blk[:, start : start + width], preferred_element_type=jnp.float32
    )


def gather_kernel(n_tok, kv_masks, q_masks, order_own, order_other, *refs):
    _, i, _, _ = place()
    toks, refs = refs[:n_tok], refs[n_tok:]
    both, refs = refs[: len(q_masks)], refs[len(q_masks) :]
    kvs, refs = refs[: len(kv_masks)], refs[len(kv_masks) :]
    rope, rows, kv_sum, q_sum, spin = refs
    block = toks[0].shape[0]
    for n, tok in enumerate(toks):
        rows[n * block : (n + 1) * block, :] = tok[...]
    for k, (nat, _, _) in enumerate(sources(order_own, order_other)):
        spin[k] = rope[nat]
    width = both[0].shape[1]
    acc = None
    for blk, mask in zip(both, q_masks):
        part = product(rows, i ^ mask, blk, 0, width)
        acc = part if acc is None else acc + part
    q_sum[...] = acc[:, HD:]
    acc = acc[:, :HD]
    for blk, mask in zip(kvs, kv_masks):
        acc = acc + product(rows, i ^ mask, blk, 0, HD)
    kv_sum[...] = acc


def gather(toks, both, q_masks, kvs, kv_masks, orders, rope):
    smem = pl.BlockSpec(memory_space=pltpu.SMEM)
    vmem = pl.BlockSpec(memory_space=pltpu.VMEM)
    block, width = toks[0].shape
    rows = block * len(toks)
    q_width = both[0].shape[1] - HD
    args = list(toks) + list(both) + list(kvs) + [rope]
    return pl.pallas_call(
        functools.partial(gather_kernel, len(toks), kv_masks, q_masks),
        out_shape=[
            jax.ShapeDtypeStruct((rows, width), jnp.bfloat16),
            jax.ShapeDtypeStruct((rows, HD), jnp.float32),
            jax.ShapeDtypeStruct((rows, q_width), jnp.float32),
            jax.ShapeDtypeStruct((len(toks),) + rope.shape[1:], jnp.float32),
        ],
        in_specs=[smem] * 2 + [vmem] * len(args),
        out_specs=[vmem] * 4,
        compiler_params=VMEM,
        cost_estimate=COST,
        name="gather_rows",
    )(*orders, *args)


def project_kernel(masks, mode, ahead, order_own, order_other, rows, acc_ref, *refs):
    _, i, b, _ = place()
    blks, refs = refs[: len(masks)], refs[len(masks) :]
    acc = acc_ref[...]
    depth = blks[0].shape[0]
    for blk, mask in zip(blks, masks):
        index = 0 if rows.shape[1] == depth else i ^ mask
        acc = acc + product(rows, index, blk, 0, blk.shape[1])
    if mode == "part":
        refs[0][...] = acc
        if ahead is not None:
            cols = pl.ds(pl.multiple_of((i ^ ahead) * depth, depth), depth)
            refs[1][...] = rows[:, cols]
        return
    spin, keep, give = refs
    block, heads = keep.shape[1], keep.shape[2] // HD
    for k, (_, kept, spot) in enumerate(sources(order_own, order_other)):
        cos, sin = spin[k, 0], spin[k, 1]
        tiles = []
        for h in range(heads):
            v = acc[k * block : (k + 1) * block, h * HD : (h + 1) * HD]
            r = v * cos + pltpu.roll(v, HD // 2, 1) * sin
            if mode == "key_value":
                r = jnp.where(b == 0, r, v)
            tiles.append(r.astype(jnp.bfloat16))
        value = tiles[0] if heads == 1 else jnp.concatenate(tiles, axis=1)

        @pl.when(kept)
        def _():
            keep[spot] = value

        @pl.when(jnp.logical_not(kept))
        def _():
            give[spot] = value


def project(mode, rows, acc, blks, masks, orders, spin=None, ahead=None):
    smem = pl.BlockSpec(memory_space=pltpu.SMEM)
    vmem = pl.BlockSpec(memory_space=pltpu.VMEM)
    width = blks[0].shape[1]
    args = [rows, acc] + list(blks) + ([] if spin is None else [spin])
    if mode == "part":
        out_shape = [jax.ShapeDtypeStruct(acc.shape, jnp.float32)]
        if ahead is not None:
            out_shape.append(jax.ShapeDtypeStruct((rows.shape[0], blks[0].shape[0]), jnp.bfloat16))
    else:
        blocks, _, block, _ = spin.shape
        out_shape = [jax.ShapeDtypeStruct((blocks // 2, block, width), jnp.bfloat16)] * 2
    return pl.pallas_call(
        functools.partial(project_kernel, masks, mode, ahead),
        out_shape=out_shape,
        in_specs=[smem] * 2 + [vmem] * len(args),
        out_specs=[vmem] * len(out_shape),
        compiler_params=VMEM,
        cost_estimate=COST,
    )(*orders, *args)


def cut_kernel(w_query, w_key, w_value, near, kv_same, q_same, kv_other, q_other, sems):
    x, _, b, _ = place()
    q_cols = q_other.shape[1]
    here = pl.ds(pl.multiple_of(x * HD, HD), HD)
    kv_near = near.at[:, :HD]

    def query(parity):
        return w_query.at[:, pl.ds(pl.multiple_of((x * 2 + parity) * q_cols, q_cols), q_cols)]

    copies = [
        pltpu.make_async_copy(query(b), near.at[:, HD:], sems.at[2]),
        pltpu.make_async_copy(query(b), q_same, sems.at[5]),
        pltpu.make_async_copy(query(1 - b), q_other, sems.at[3]),
    ]
    even = [
        pltpu.make_async_copy(w_key.at[:, here], kv_near, sems.at[0]),
        pltpu.make_async_copy(w_key.at[:, here], kv_same, sems.at[4]),
        pltpu.make_async_copy(w_value.at[:, here], kv_other, sems.at[1]),
    ]
    odd = [
        pltpu.make_async_copy(w_value.at[:, here], kv_near, sems.at[0]),
        pltpu.make_async_copy(w_value.at[:, here], kv_same, sems.at[4]),
        pltpu.make_async_copy(w_key.at[:, here], kv_other, sems.at[1]),
    ]

    @pl.when(b == 0)
    def _():
        for copy in even:
            copy.start()

    @pl.when(b != 0)
    def _():
        for copy in odd:
            copy.start()

    for copy in copies:
        copy.start()
    for copy in even + copies:
        copy.wait()


def cut(w_query, w_key, w_value, q_cols):
    depth = w_query.shape[0]
    return pl.pallas_call(
        cut_kernel,
        out_shape=[
            jax.ShapeDtypeStruct((depth, HD + q_cols), jnp.bfloat16),
        ]
        + [
            jax.ShapeDtypeStruct((depth, HD), jnp.bfloat16),
            jax.ShapeDtypeStruct((depth, q_cols), jnp.bfloat16),
        ]
        * 2,
        in_specs=[pl.BlockSpec(memory_space=pl.ANY)] * 3,
        out_specs=[pl.BlockSpec(memory_space=pltpu.VMEM)] * 5,
        scratch_shapes=[pltpu.SemaphoreType.DMA((6,))],
        compiler_params=CUT,
        cost_estimate=COST,
        name="cut",
    )(w_query, w_key, w_value)


def norm_kernel(tok, gain, normed):
    v = tok[...].astype(jnp.float32)
    scale = lax.rsqrt(jnp.mean(v * v, axis=-1, keepdims=True) + 1e-05)
    normed[...] = (v * scale * gain[...]).astype(jnp.bfloat16)


def norm(tokens, gain, block, index, params=VMEM):
    width = tokens.shape[1]
    return pl.pallas_call(
        norm_kernel,
        grid=(1,),
        out_shape=jax.ShapeDtypeStruct((block, width), jnp.bfloat16),
        in_specs=[
            pl.BlockSpec((block, width), lambda n: (index(), 0)),
            pl.BlockSpec((1, width), lambda n: (0, 0)),
        ],
        out_specs=pl.BlockSpec((block, width), lambda n: (0, 0)),
        compiler_params=params,
        cost_estimate=COST,
        name="norm",
    )(tokens, gain)


def attend_kernel(kv_masks, scale, first, *refs):
    x, i, b, _ = place()
    order_own, docs_own, order_other, docs_other, query_ref = refs[:5]
    blocks, block, width = query_ref.shape
    heads = width // HD
    base = i - 2 * b

    def table(own, other, index):
        return jnp.where(x == b, own[index], other[index])

    def natural(mask, k):
        return table(order_own, order_other, ((base ^ mask) + 2 * (k // 2)) * 2 + k % 2)

    if first:
        kvs, (out, key_ref, value_ref) = refs[5:-3], refs[-3:]
        for n, mask in enumerate(kv_masks):
            for k in range(blocks):
                kept, got = kvs[2 * n][k], kvs[2 * n + 1][k]
                nat = natural(mask, k)
                key_ref[nat] = jnp.where(b == 0, kept, got)
                value_ref[nat] = jnp.where(b == 0, got, kept)
    else:
        key_ref, value_ref, out = refs[5:]
    total_blocks = key_ref.shape[0]
    window = total_blocks // 2
    lane = lax.broadcasted_iota(jnp.int32, (1, window * block), 1)
    row = lax.broadcasted_iota(jnp.int32, (block, 1), 0)
    for k in range(blocks):
        nat = natural(0, k)
        doc = table(docs_own, docs_other, nat)
        start = jnp.maximum(nat - (window - 1), 0)
        opening = jnp.int32(0)
        for n in range(total_blocks):
            opening += (table(docs_own, docs_other, n) < doc).astype(jnp.int32)
        key = key_ref[pl.ds(start, window)].reshape(window * block, HD)
        value = value_ref[pl.ds(start, window)].reshape(window * block, HD)
        query = jnp.concatenate([query_ref[k, :, h * HD : (h + 1) * HD] for h in range(heads)], axis=0)
        scores = lax.dot_general(
            query, key, (((1,), (1,)), ((), ())), preferred_element_type=jnp.float32
        )
        key_pos = start * block + lane
        allowed = (key_pos <= nat * block + row) & (key_pos >= opening * block)
        bias = jnp.where(allowed, 0.0, -jnp.inf)
        scores = scores + jnp.concatenate([bias] * heads, axis=0)
        row_max = jnp.max(scores, axis=-1, keepdims=True)
        weights = jnp.exp2((scores - row_max) * (scale * math.log2(math.e)))
        total = jnp.sum(weights, axis=-1, keepdims=True)
        mixed = jnp.dot(weights.astype(jnp.bfloat16), value, preferred_element_type=jnp.float32) / total
        out[k * block : (k + 1) * block, :] = jnp.concatenate(
            [mixed[h * block : (h + 1) * block].astype(jnp.bfloat16) for h in range(heads)], axis=1
        )


def attend(first, tables, query, kvs, kv_masks):
    blocks, block, width = query.shape
    smem = pl.BlockSpec(memory_space=pltpu.SMEM)
    vmem = pl.BlockSpec(memory_space=pltpu.VMEM)
    out_shape = [jax.ShapeDtypeStruct((blocks * block, width), jnp.bfloat16)]
    if first:
        out_shape += [jax.ShapeDtypeStruct((tables[0].shape[0], block, HD), jnp.bfloat16)] * 2
    return pl.pallas_call(
        functools.partial(attend_kernel, kv_masks, 1.0 / math.sqrt(HD), first),
        out_shape=out_shape,
        in_specs=[smem] * len(tables) + [vmem] * (1 + len(kvs)),
        out_specs=[vmem] * len(out_shape),
        compiler_params=VMEM,
        cost_estimate=COST,
        name="attend_first" if first else "attend_second",
    )(*tables, query, *kvs)


def per_device(
    tokens, norm_gain, w_query, w_key, w_value, block_order, block_docs, head_owner, prev_kv
):
    groups, n_seq = lax.axis_size("groups"), lax.axis_size("seq")
    planes = n_seq // 2
    rows_dev = tokens.shape[0]
    slots = block_order.shape[0] // n_seq
    block = rows_dev // slots
    x, _, b, c = place()

    def swap_seq(v, mask):
        return lax.ppermute(v, "seq", [(j, j ^ mask) for j in range(n_seq)])

    def swap_group(v):
        return lax.ppermute(v, "groups", [(j, j ^ 1) for j in range(groups)])

    def swap_core(v):
        return lax.ppermute(v, "dec", [(0, 1), (1, 0)])

    smem = pl.BlockSpec(memory_space=pltpu.SMEM)
    vmem = pl.BlockSpec(memory_space=pltpu.VMEM)
    gain = norm_gain[None, :]
    half = norm(tokens, gain, block, lambda: place()[3], None)
    rest = norm(tokens, gain, block, lambda: 1 - place()[3])

    n_blocks = block_order.shape[0]
    frequency = 500000.0 ** (-jnp.arange(HD // 2, dtype=jnp.float32) / (HD // 2))
    angles = jnp.arange(n_blocks * block, dtype=jnp.int32).astype(jnp.float32)[:, None] * frequency[None, :]
    cosines, sines = jnp.cos(angles), jnp.sin(angles)
    cos_table = jnp.concatenate([cosines, cosines], -1).reshape(n_blocks, 1, block, HD)
    sin_table = jnp.concatenate([-sines, sines], -1).reshape(n_blocks, 1, block, HD)
    rope = jnp.concatenate([cos_table, sin_table], axis=1)

    own_tables = jnp.concatenate([block_order, block_docs])
    own_tables, rope = lax.optimization_barrier((own_tables, rope))
    other_tables = swap_group(own_tables)
    order_other = other_tables[: block_order.shape[0]]
    docs_other = other_tables[block_order.shape[0] :]

    q_cols = w_query.shape[1] // 4
    near, kv_same, q_same, kv_other, q_other = cut(w_query, w_key, w_value, q_cols)
    kv_cols, q_parts = [kv_same, kv_other], [q_same, q_other]

    tok_z = swap_seq(half, 2)
    tok_x = swap_group(half)
    both_y0 = swap_seq(near, 1)
    kv_z = [near] + [swap_seq(kv_cols[d % 2], 2 * d) for d in range(1, planes)]
    q_z = [near] + [swap_seq(q_parts[d % 2], 2 * d) for d in range(1, planes)]
    kv_y = [both_y0] + [swap_seq(kv_z[d], 1) for d in range(1, planes)]
    q_y = [both_y0] + [swap_seq(q_z[d], 1) for d in range(1, planes)]
    tok_xz = swap_group(tok_z)
    toks = [half, tok_z, tok_x, tok_xz, rest] + [swap_core(t) for t in (tok_z, tok_x, tok_xz)]

    orders = (block_order, order_other)

    rows, kv_acc, q_acc, spin = gather(
        toks, (near, both_y0), (0, 1), kv_z[1:], [2 * d for d in range(1, planes)], orders, rope
    )
    kv_keep, kv_give = project(
        "key_value", rows, kv_acc, kv_y[1:], [2 * d + 1 for d in range(1, planes)], orders, spin
    )
    kvx_z = [kv_keep] + [swap_seq(kv_give if d % 2 else kv_keep, 2 * d) for d in range(1, planes)]
    kvx_y = [swap_seq(kvx_z[d], 1) for d in range(planes)]
    pairs = range(0, planes, 2)
    kv_masks = [2 * d for d in pairs] + [2 * d + 1 for d in pairs]
    kv_all = [v for part in (kvx_z, kvx_y) for v in part]

    last = 2 if planes > 2 else 1
    firsts = [(q_z[d], 2 * d) for d in range(1, planes) if d != last or planes == 2]
    thens = [] if planes == 2 else [(q_z[last], 2 * last)]
    thens += [(q_y[d], 2 * d + 1) for d in range(1, planes) if d != last]
    left = rows
    for n, part in enumerate((firsts, thens)):
        if part:
            done = project(
                "part", rows, q_acc, [v for v, _ in part], [m for _, m in part], orders,
                ahead=2 * last + 1 if n else None,
            )
            q_acc = done[0]
            left = done[1] if n else left
    q_keep, q_give = project(
        "query", left, q_acc, [q_y[last]], [2 * last + 1], orders, spin
    )
    q_got = swap_seq(q_give, 2)

    tables = (block_order, block_docs, order_other, docs_other)
    att_keep, key_all, value_all = attend(True, tables, q_keep, kv_all, kv_masks)
    (att_got,) = attend(False, tables, q_got, (key_all, value_all), kv_masks)
    att = [att_keep, att_got]
    attended = jnp.concatenate(
        [jnp.where(b == 0, att[0], att[1]), jnp.where(b == 0, att[1], att[0])], axis=1
    )

    first_rows = attended[:rows_dev]
    second_rows = attended[rows_dev:]
    at_b = jnp.where(b == 0, first_rows, second_rows)
    at_other = jnp.where(b == 0, second_rows, first_rows)
    perm_a, perm_b = [], []
    for gg in range(groups):
        for ii in range(n_seq):
            src = gg * n_seq + ii
            if gg % 2 == (ii // 2) % 2:
                perm_a.append((src, gg * n_seq + (ii ^ 2)))
            else:
                perm_a.append((src, (gg ^ 1) * n_seq + ii))
                perm_b.append((src, (gg ^ 1) * n_seq + (ii ^ 2)))
    home = x == b
    from_a = lax.ppermute(jnp.where(home, at_other, at_b), ("groups", "seq"), perm_a)
    from_b = lax.ppermute(at_other, ("groups", "seq"), perm_b)
    same_x = jnp.where(home, at_b, from_a)
    cross_x = jnp.where(home, from_a, from_b)
    out = jnp.concatenate(
        [jnp.where(x == 0, same_x, cross_x), jnp.where(x == 0, cross_x, same_x)], axis=1
    )

    head_count = prev_kv.shape[2]
    selector = (head_owner[:, None] == jnp.arange(head_count, dtype=jnp.int32)[None, :]).astype(
        jnp.bfloat16
    )
    ordered = jnp.einsum(
        "tcjd,sj->tcsd", prev_kv, selector, preferred_element_type=jnp.float32
    ).astype(jnp.bfloat16)
    per_dec = head_count // 2
    stay = jnp.where(c == 0, ordered[:, :, :per_dec], ordered[:, :, per_dec:])
    leave = jnp.where(c == 0, ordered[:, :, per_dec:], ordered[:, :, :per_dec])
    come = swap_core(leave)
    decode_cache = jnp.concatenate(
        [jnp.where(c == 0, stay, come), jnp.where(c == 0, come, stay)], axis=0
    )
    return (out, decode_cache)


def solution(mesh):
    in_specs = (
        P(("groups", "seq"), None),
        P(),
        P("seq", "dec"),
        P("seq", "dec"),
        P("seq", "dec"),
        P("groups"),
        P("groups"),
        P("groups"),
        P(("groups", "seq", "dec"), None, None, None),
    )
    out_specs = (P(("groups", "seq"), "dec"), P(("groups", "seq"), None, "dec", None))

    return jax.shard_map(
        per_device, mesh=mesh, in_specs=in_specs, out_specs=out_specs, check_vma=False
    )
```

```python
import functools
import math

import jax
import jax.numpy as jnp
from jax import lax
from jax.experimental import pallas as pl
from jax.experimental.pallas import tpu as pltpu
from jax.sharding import PartitionSpec as P


HD = 128
VMEM = pltpu.CompilerParams(vmem_limit_bytes=16 * 2**20)
CUT = None
COST = pl.CostEstimate(flops=1024, bytes_accessed=1024, transcendentals=0)


def place():
    g, i, c = lax.axis_index("groups"), lax.axis_index("seq"), lax.axis_index("dec")
    return g % 2, i, lax.div(i, 2) % 2, c


def sources(tables=None):
    x, i, b, c = place()
    found = []
    for k in range(8):
        grp = x if k % 4 < 2 else 1 - x
        par = b if k % 4 in (0, 2) else 1 - b
        part = c if k < 4 else 1 - c
        nat = None
        if tables is not None:
            nat = tables[0 if k % 4 < 2 else 1][(i - 2 * b + 2 * par) * 2 + part]
        found.append((nat, grp == b, par * 2 + part))
    return found


def product(lhs_ref, index, blk, start, width):
    depth = blk.shape[0]
    cols = pl.ds(pl.multiple_of(index * depth, depth), depth)
    return jnp.dot(
        lhs_ref[:, cols], blk[:, start : start + width], preferred_element_type=jnp.float32
    )


def gather_kernel(n_tok, kv_masks, q_masks, order_own, order_other, *refs):
    _, i, _, _ = place()
    toks, refs = refs[:n_tok], refs[n_tok:]
    both, refs = refs[: len(q_masks)], refs[len(q_masks) :]
    kvs, refs = refs[: len(kv_masks)], refs[len(kv_masks) :]
    rope, rows, kv_sum, q_sum, spin = refs
    block = toks[0].shape[0]
    for n, tok in enumerate(toks):
        rows[n * block : (n + 1) * block, :] = tok[...]
    for k, (nat, _, _) in enumerate(sources((order_own, order_other))):
        spin[k] = rope[nat]
    width = both[0].shape[1]
    acc = None
    for blk, mask in zip(both, q_masks):
        part = product(rows, i ^ mask, blk, 0, width)
        acc = part if acc is None else acc + part
    q_sum[...] = acc[:, HD:]
    acc = acc[:, :HD]
    for blk, mask in zip(kvs, kv_masks):
        acc = acc + product(rows, i ^ mask, blk, 0, HD)
    kv_sum[...] = acc


def gather(toks, both, q_masks, kvs, kv_masks, orders, rope):
    smem = pl.BlockSpec(memory_space=pltpu.SMEM)
    vmem = pl.BlockSpec(memory_space=pltpu.VMEM)
    block, width = toks[0].shape
    rows = block * len(toks)
    q_width = both[0].shape[1] - HD
    args = list(toks) + list(both) + list(kvs) + [rope]
    return pl.pallas_call(
        functools.partial(gather_kernel, len(toks), kv_masks, q_masks),
        out_shape=[
            jax.ShapeDtypeStruct((rows, width), jnp.bfloat16),
            jax.ShapeDtypeStruct((rows, HD), jnp.float32),
            jax.ShapeDtypeStruct((rows, q_width), jnp.float32),
            jax.ShapeDtypeStruct((len(toks),) + rope.shape[1:], jnp.float32),
        ],
        in_specs=[smem] * 2 + [vmem] * len(args),
        out_specs=[vmem] * 4,
        compiler_params=VMEM,
        cost_estimate=COST,
        name="gather_rows",
    )(*orders, *args)


def project_kernel(masks, mode, ahead, *refs):
    _, i, b, _ = place()
    rows, acc_ref = refs[:2]
    blks, refs = refs[2 : 2 + len(masks)], refs[2 + len(masks) :]
    acc = acc_ref[...]
    depth = blks[0].shape[0]
    for blk, mask in zip(blks, masks):
        index = 0 if rows.shape[1] == depth else i ^ mask
        acc = acc + product(rows, index, blk, 0, blk.shape[1])
    if mode == "part":
        refs[0][...] = acc
        if ahead is not None:
            cols = pl.ds(pl.multiple_of((i ^ ahead) * depth, depth), depth)
            refs[1][...] = rows[:, cols]
        return
    spin, keep, give = refs
    block, heads = keep.shape[1], keep.shape[2] // HD
    for k, (_, kept, spot) in enumerate(sources()):
        cos, sin = spin[k, 0], spin[k, 1]
        tiles = []
        for h in range(heads):
            v = acc[k * block : (k + 1) * block, h * HD : (h + 1) * HD]
            r = v * cos + pltpu.roll(v, HD // 2, 1) * sin
            if mode == "key_value":
                r = jnp.where(b == 0, r, v)
            tiles.append(r.astype(jnp.bfloat16))
        value = tiles[0] if heads == 1 else jnp.concatenate(tiles, axis=1)

        @pl.when(kept)
        def _():
            keep[spot] = value

        @pl.when(jnp.logical_not(kept))
        def _():
            give[spot] = value


def project(mode, rows, acc, blks, masks, spin=None, ahead=None):
    vmem = pl.BlockSpec(memory_space=pltpu.VMEM)
    width = blks[0].shape[1]
    args = [rows, acc] + list(blks) + ([] if spin is None else [spin])
    if mode == "part":
        out_shape = [jax.ShapeDtypeStruct(acc.shape, jnp.float32)]
        if ahead is not None:
            out_shape.append(jax.ShapeDtypeStruct((rows.shape[0], blks[0].shape[0]), jnp.bfloat16))
    else:
        blocks, _, block, _ = spin.shape
        out_shape = [jax.ShapeDtypeStruct((blocks // 2, block, width), jnp.bfloat16)] * 2
    return pl.pallas_call(
        functools.partial(project_kernel, masks, mode, ahead),
        out_shape=out_shape,
        in_specs=[vmem] * len(args),
        out_specs=[vmem] * len(out_shape),
        compiler_params=VMEM,
        cost_estimate=COST,
    )(*args)


def cut_kernel(w_query, w_key, w_value, near, kv_same, q_same, kv_other, q_other, sems):
    x, _, b, _ = place()
    q_cols = q_other.shape[1]
    here = pl.ds(pl.multiple_of(x * HD, HD), HD)
    kv_near = near.at[:, :HD]

    def query(parity):
        return w_query.at[:, pl.ds(pl.multiple_of((x * 2 + parity) * q_cols, q_cols), q_cols)]

    copies = [
        pltpu.make_async_copy(query(b), near.at[:, HD:], sems.at[2]),
        pltpu.make_async_copy(query(b), q_same, sems.at[5]),
        pltpu.make_async_copy(query(1 - b), q_other, sems.at[3]),
    ]
    even = [
        pltpu.make_async_copy(w_key.at[:, here], kv_near, sems.at[0]),
        pltpu.make_async_copy(w_key.at[:, here], kv_same, sems.at[4]),
        pltpu.make_async_copy(w_value.at[:, here], kv_other, sems.at[1]),
    ]
    odd = [
        pltpu.make_async_copy(w_value.at[:, here], kv_near, sems.at[0]),
        pltpu.make_async_copy(w_value.at[:, here], kv_same, sems.at[4]),
        pltpu.make_async_copy(w_key.at[:, here], kv_other, sems.at[1]),
    ]

    @pl.when(b == 0)
    def _():
        for copy in even:
            copy.start()

    @pl.when(b != 0)
    def _():
        for copy in odd:
            copy.start()

    for copy in copies:
        copy.start()
    for copy in even + copies:
        copy.wait()


def cut(w_query, w_key, w_value, q_cols):
    depth = w_query.shape[0]
    return pl.pallas_call(
        cut_kernel,
        out_shape=[
            jax.ShapeDtypeStruct((depth, HD + q_cols), jnp.bfloat16),
        ]
        + [
            jax.ShapeDtypeStruct((depth, HD), jnp.bfloat16),
            jax.ShapeDtypeStruct((depth, q_cols), jnp.bfloat16),
        ]
        * 2,
        in_specs=[pl.BlockSpec(memory_space=pl.ANY)] * 3,
        out_specs=[pl.BlockSpec(memory_space=pltpu.VMEM)] * 5,
        scratch_shapes=[pltpu.SemaphoreType.DMA((6,))],
        compiler_params=CUT,
        cost_estimate=COST,
        name="cut",
    )(w_query, w_key, w_value)


def norm_kernel(tok, gain, normed):
    v = tok[...].astype(jnp.float32)
    scale = lax.rsqrt(jnp.mean(v * v, axis=-1, keepdims=True) + 1e-05)
    normed[...] = (v * scale * gain[...]).astype(jnp.bfloat16)


def norm(tokens, gain, block, index, params=VMEM):
    width = tokens.shape[1]
    return pl.pallas_call(
        norm_kernel,
        grid=(1,),
        out_shape=jax.ShapeDtypeStruct((block, width), jnp.bfloat16),
        in_specs=[
            pl.BlockSpec((block, width), lambda n: (index(), 0)),
            pl.BlockSpec((1, width), lambda n: (0, 0)),
        ],
        out_specs=pl.BlockSpec((block, width), lambda n: (0, 0)),
        compiler_params=params,
        cost_estimate=COST,
        name="norm",
    )(tokens, gain)


def attend_kernel(kv_masks, scale, first, own_tables, other_tables, query_ref, *refs):
    x, i, b, _ = place()
    blocks, block, width = query_ref.shape
    heads = width // HD
    base = i - 2 * b

    def table(index):
        return jnp.where(x == b, own_tables[index], other_tables[index])

    def natural(mask, k):
        return table(((base ^ mask) + 2 * (k // 2)) * 2 + k % 2)

    if first:
        kvs, (out, key_ref, value_ref) = refs[:-3], refs[-3:]
        for n, mask in enumerate(kv_masks):
            for k in range(blocks):
                kept, got = kvs[2 * n][k], kvs[2 * n + 1][k]
                nat = natural(mask, k)
                key_ref[nat] = jnp.where(b == 0, kept, got)
                value_ref[nat] = jnp.where(b == 0, got, kept)
    else:
        key_ref, value_ref, out = refs
    total_blocks = key_ref.shape[0]
    window = total_blocks // 2
    lane = lax.broadcasted_iota(jnp.int32, (1, window * block), 1)
    row = lax.broadcasted_iota(jnp.int32, (block, 1), 0)
    docs = [table(total_blocks + n) for n in range(total_blocks)]
    tasks = []
    for k in range(blocks):
        nat = natural(0, k)
        doc = table(total_blocks + nat)
        opening = jnp.int32(0)
        for other in docs:
            opening += (other < doc).astype(jnp.int32)
        start = jnp.maximum(nat - (window - 1), 0)
        key = key_ref[pl.ds(start, window)].reshape(window * block, HD)
        query = jnp.concatenate([query_ref[k, :, h * HD : (h + 1) * HD] for h in range(heads)], axis=0)
        scores = lax.dot_general(
            query, key, (((1,), (1,)), ((), ())), preferred_element_type=jnp.float32
        )
        tasks.append((nat, opening, start, scores))
    shares = []
    for nat, opening, start, scores in tasks:
        key_pos = start * block + lane
        allowed = (key_pos <= nat * block + row) & (key_pos >= opening * block)
        bias = jnp.where(allowed, 0.0, -jnp.inf)
        scores = scores + jnp.concatenate([bias] * heads, axis=0)
        row_max = jnp.max(scores, axis=-1, keepdims=True)
        weights = jnp.exp2((scores - row_max) * (scale * math.log2(math.e)))
        shares.append((weights.astype(jnp.bfloat16), jnp.sum(weights, axis=-1, keepdims=True)))
    for k, ((_, _, start, _), (weights, total)) in enumerate(zip(tasks, shares)):
        value = value_ref[pl.ds(start, window)].reshape(window * block, HD)
        mixed = jnp.dot(weights, value, preferred_element_type=jnp.float32) / total
        out[k * block : (k + 1) * block, :] = jnp.concatenate(
            [mixed[h * block : (h + 1) * block].astype(jnp.bfloat16) for h in range(heads)], axis=1
        )


def attend(first, tables, query, kvs, kv_masks):
    blocks, block, width = query.shape
    smem = pl.BlockSpec(memory_space=pltpu.SMEM)
    vmem = pl.BlockSpec(memory_space=pltpu.VMEM)
    out_shape = [jax.ShapeDtypeStruct((blocks * block, width), jnp.bfloat16)]
    if first:
        out_shape += [jax.ShapeDtypeStruct((tables[0].shape[0] // 2, block, HD), jnp.bfloat16)] * 2
    return pl.pallas_call(
        functools.partial(attend_kernel, kv_masks, 1.0 / math.sqrt(HD), first),
        out_shape=out_shape,
        in_specs=[smem] * len(tables) + [vmem] * (1 + len(kvs)),
        out_specs=[vmem] * len(out_shape),
        compiler_params=VMEM,
        cost_estimate=COST,
        name="attend_first" if first else "attend_second",
    )(*tables, query, *kvs)


def per_device(
    tokens, norm_gain, w_query, w_key, w_value, block_order, block_docs, head_owner, prev_kv
):
    groups, n_seq = lax.axis_size("groups"), lax.axis_size("seq")
    planes = n_seq // 2
    rows_dev = tokens.shape[0]
    slots = block_order.shape[0] // n_seq
    block = rows_dev // slots
    x, _, b, c = place()

    def swap_seq(v, mask):
        return lax.ppermute(v, "seq", [(j, j ^ mask) for j in range(n_seq)])

    def swap_group(v):
        return lax.ppermute(v, "groups", [(j, j ^ 1) for j in range(groups)])

    def swap_core(v):
        return lax.ppermute(v, "dec", [(0, 1), (1, 0)])

    smem = pl.BlockSpec(memory_space=pltpu.SMEM)
    vmem = pl.BlockSpec(memory_space=pltpu.VMEM)
    gain = norm_gain[None, :]
    half = norm(tokens, gain, block, lambda: place()[3], None)
    rest = norm(tokens, gain, block, lambda: 1 - place()[3])

    n_blocks = block_order.shape[0]
    frequency = 500000.0 ** (-jnp.arange(HD // 2, dtype=jnp.float32) / (HD // 2))
    angles = jnp.arange(n_blocks * block, dtype=jnp.int32).astype(jnp.float32)[:, None] * frequency[None, :]
    cosines, sines = jnp.cos(angles), jnp.sin(angles)
    cos_table = jnp.concatenate([cosines, cosines], -1).reshape(n_blocks, 1, block, HD)
    sin_table = jnp.concatenate([-sines, sines], -1).reshape(n_blocks, 1, block, HD)
    rope = jnp.concatenate([cos_table, sin_table], axis=1)

    own_tables = jnp.concatenate([block_order, block_docs])
    own_tables, rope = lax.optimization_barrier((own_tables, rope))
    other_tables = swap_group(own_tables)

    q_cols = w_query.shape[1] // 4
    near, kv_same, q_same, kv_other, q_other = cut(w_query, w_key, w_value, q_cols)
    kv_cols, q_parts = [kv_same, kv_other], [q_same, q_other]

    tok_z = swap_seq(half, 2)
    tok_x = swap_group(half)
    both_y0 = swap_seq(near, 1)
    kv_z = [near] + [swap_seq(kv_cols[d % 2], 2 * d) for d in range(1, planes)]
    q_z = [near] + [swap_seq(q_parts[d % 2], 2 * d) for d in range(1, planes)]
    kv_y = [both_y0] + [swap_seq(kv_z[d], 1) for d in range(1, planes)]
    q_y = [both_y0] + [swap_seq(q_z[d], 1) for d in range(1, planes)]
    tok_xz = swap_group(tok_z)
    toks = [half, tok_z, tok_x, tok_xz, rest] + [swap_core(t) for t in (tok_z, tok_x, tok_xz)]

    orders = (own_tables, other_tables)

    rows, kv_acc, q_acc, spin = gather(
        toks, (near, both_y0), (0, 1), kv_z[1:], [2 * d for d in range(1, planes)], orders, rope
    )
    kv_keep, kv_give = project(
        "key_value", rows, kv_acc, kv_y[1:], [2 * d + 1 for d in range(1, planes)], spin
    )
    kvx_z = [kv_keep] + [swap_seq(kv_give if d % 2 else kv_keep, 2 * d) for d in range(1, planes)]
    kvx_y = [swap_seq(kvx_z[d], 1) for d in range(planes)]
    pairs = range(0, planes, 2)
    kv_masks = [2 * d for d in pairs] + [2 * d + 1 for d in pairs]
    kv_all = [v for part in (kvx_z, kvx_y) for v in part]

    last = 2 if planes > 2 else 1
    firsts = [(q_z[d], 2 * d) for d in range(1, planes) if d != last or planes == 2]
    thens = [] if planes == 2 else [(q_z[last], 2 * last)]
    thens += [(q_y[d], 2 * d + 1) for d in range(1, planes) if d != last]
    left = rows
    for n, part in enumerate((firsts, thens)):
        if part:
            done = project(
                "part", rows, q_acc, [v for v, _ in part], [m for _, m in part],
                ahead=2 * last + 1 if n else None,
            )
            q_acc = done[0]
            left = done[1] if n else left
    q_keep, q_give = project(
        "query", left, q_acc, [q_y[last]], [2 * last + 1], spin
    )
    q_got = swap_seq(q_give, 2)

    tables = orders
    att_keep, key_all, value_all = attend(True, tables, q_keep, kv_all, kv_masks)
    (att_got,) = attend(False, tables, q_got, (key_all, value_all), kv_masks)
    att = [att_keep, att_got]
    attended = jnp.concatenate(
        [jnp.where(b == 0, att[0], att[1]), jnp.where(b == 0, att[1], att[0])], axis=1
    )

    first_rows = attended[:rows_dev]
    second_rows = attended[rows_dev:]
    at_b = jnp.where(b == 0, first_rows, second_rows)
    at_other = jnp.where(b == 0, second_rows, first_rows)
    perm_a, perm_b = [], []
    for gg in range(groups):
        for ii in range(n_seq):
            src = gg * n_seq + ii
            if gg % 2 == (ii // 2) % 2:
                perm_a.append((src, gg * n_seq + (ii ^ 2)))
            else:
                perm_a.append((src, (gg ^ 1) * n_seq + ii))
                perm_b.append((src, (gg ^ 1) * n_seq + (ii ^ 2)))
    home = x == b
    from_a = lax.ppermute(jnp.where(home, at_other, at_b), ("groups", "seq"), perm_a)
    from_b = lax.ppermute(at_other, ("groups", "seq"), perm_b)
    same_x = jnp.where(home, at_b, from_a)
    cross_x = jnp.where(home, from_a, from_b)
    out = jnp.concatenate(
        [jnp.where(x == 0, same_x, cross_x), jnp.where(x == 0, cross_x, same_x)], axis=1
    )

    head_count = prev_kv.shape[2]
    selector = (head_owner[:, None] == jnp.arange(head_count, dtype=jnp.int32)[None, :]).astype(
        jnp.bfloat16
    )
    ordered = jnp.einsum(
        "tcjd,sj->tcsd", prev_kv, selector, preferred_element_type=jnp.float32
    ).astype(jnp.bfloat16)
    per_dec = head_count // 2
    stay = jnp.where(c == 0, ordered[:, :, :per_dec], ordered[:, :, per_dec:])
    leave = jnp.where(c == 0, ordered[:, :, per_dec:], ordered[:, :, :per_dec])
    come = swap_core(leave)
    decode_cache = jnp.concatenate(
        [jnp.where(c == 0, stay, come), jnp.where(c == 0, come, stay)], axis=0
    )
    return (out, decode_cache)


def solution(mesh):
    in_specs = (
        P(("groups", "seq"), None),
        P(),
        P("seq", "dec"),
        P("seq", "dec"),
        P("seq", "dec"),
        P("groups"),
        P("groups"),
        P("groups"),
        P(("groups", "seq", "dec"), None, None, None),
    )
    out_specs = (P(("groups", "seq"), "dec"), P(("groups", "seq"), None, "dec", None))

    return jax.shard_map(
        per_device, mesh=mesh, in_specs=in_specs, out_specs=out_specs, check_vma=False
    )
```
